32 devices in a mesh: fsdp: 4 (over x, core), ctx: 8 (over z, y).
Axes of the slice: x: 2, y: 2, z: 4, core: 2. Of those that a mesh axis runs over, the one named last changes fastest.
Arguments:
- queries: bfloat16 [4, 3072, 2560], P('fsdp', 'ctx'), may hold values from -2 to 2
- keys_rot: bfloat16 [4, 3072, 512], P('fsdp', 'ctx'), may hold values from -1 to 1
- values: bfloat16 [4, 3072, 512], P('fsdp', 'ctx'), may hold values from -6 to 6
- attention_out: bfloat16 [4, 3072, 2560], P('fsdp', 'ctx'), may hold values from -6 to 6
- grad_out: bfloat16 [4, 3072, 2560], P('fsdp', 'ctx'), may hold values from -6 to 6
- layer_input: bfloat16 [4, 3072, 2560], P('fsdp', 'ctx'), may hold values from -6 to 6
- doc_lengths: int32 [4, 7], P('fsdp'), may hold values from 1 to 768, 3072 in all within a row
Outputs:
- grad_query: bfloat16 [4, 3072, 2560], P('fsdp', 'ctx')
- grad_wk: float32 [2560, 512], P('ctx', 'fsdp')
- grad_wv: float32 [2560, 512], P('ctx', 'fsdp')
The draws below stay inside these ranges and needn't reach their ends.
Inputs may be any that keep to these rules, and one draw needn't show every extreme that they name: `doc_lengths`: each row holds the lengths of the documents of one sequence in order; they sum to 3072, and the longest is exactly 768.
All inputs are finite; a program needn't handle non-finite values.
Results may differ from the reference program's by a relative error of at most 0.0049.
Values may be sent and summed in bfloat16 or wider, within the bound.
A program may use at most 128 MiB of HBM per device.

```python
import math
import jax
import jax.numpy as jnp
import numpy as np
from jax import lax

H = 20
G = 4
HD = 128
DW = 2560
LEN = 3072
MOST = 768
NDOC = 7
NSEQ = 4


def raised(result, key, source, target, parts, factor):
    def block_of(position):
        return (jnp.arange(result.shape[position]) // (result.shape[position] // parts)).reshape((-1,) + (1,) * (result.ndim - 1 - position))

    one_side = jax.random.permutation(key, parts)[block_of(target)]
    second = (block_of(target) + parts // 2) % parts
    return jnp.where((block_of(source) == one_side) | (block_of(source) == second), factor * result, result)


def shard_levels(own_key, shape, pieces, low, high):
    loudness, own = 1.0, jax.random.fold_in(own_key, 6)
    for dim, blocks in pieces:
        steps = jnp.exp(jax.random.uniform(jax.random.fold_in(own, dim), (blocks,), jnp.float32, low / len(pieces), high / len(pieces)))
        loudness = loudness * jnp.repeat(steps, shape[dim] // blocks).reshape([-1 if axis == dim else 1 for axis in range(len(shape))])
    return loudness


def profile(count, total, most, slope):
    weights = [(1 << 20) // math.isqrt(rank ** slope) + 1 for rank in range(2, count + 1)]
    spare, given = total - most - (count - 1), [1] * (count - 1)
    while spare > 0:
        candidates = [i for i in range(count - 1) if given[i] < most]
        mass, budget = sum([weights[i] for i in candidates]), spare
        for i in candidates:
            more = min(most - given[i], max(1, budget * weights[i] // mass), spare)
            given[i] = given[i] + more
            spare = spare - more
    return np.array([most] + given)


def ragged(stream_key, number_of, total, bound, slope):
    if number_of == 2:
        one = jax.random.randint(stream_key, (), max(1, total - bound), min(bound, total - 1) + 1)
        return jnp.stack([one, total - one])
    sizes = jnp.asarray(profile(number_of, total, bound, slope), jnp.int32)
    couples = (number_of - 1) // 2
    giver, taker = sizes[1:1 + 2 * couples:2], sizes[2:2 + 2 * couples:2]
    slack = jnp.minimum(giver - 1, bound - taker)
    passed = jax.random.randint(jax.random.fold_in(stream_key, 1), (couples,), 0, 1 << 20) % (slack + 1)
    sizes = sizes.at[1:1 + 2 * couples:2].set(giver - passed).at[2:2 + 2 * couples:2].set(taker + passed)
    return sizes[jax.random.permutation(jax.random.fold_in(stream_key, 2), number_of)]


def noise(stream_key, dims, deviation, most, cuts=(), held_as=jnp.bfloat16):
    entries = deviation * jax.random.normal(stream_key, dims, jnp.float32)
    if cuts:
        entries = entries * shard_levels(stream_key, dims, cuts, -0.22, 0.18)
    return jnp.clip(entries, -most, most).astype(held_as)


def bell_draw_with(own_key, extent, spread, most, shards, heavy, kind=jnp.bfloat16):
    drawn = spread * jax.random.normal(own_key, extent, jnp.float32)
    if shards:
        drawn = drawn * shard_levels(own_key, extent, shards, -0.22, 0.18)
    return jnp.clip(raised(drawn, jax.random.fold_in(own_key, 3), *heavy), -most, most).astype(kind)


def setup_inputs(seed: int = 0) -> dict:
    key_of = jax.random.split(jax.random.key(seed), 8)
    queries = jnp.clip(jax.random.uniform(key_of[0], (NSEQ, LEN, H * HD), jnp.float32, -2.0, 2.0) * shard_levels(key_of[0], (NSEQ, LEN, H * HD), ((0, 4), (1, 8)), -0.4, 0.0), -2.0, 2.0).astype(jnp.bfloat16)
    keys_rot = jnp.clip(jax.random.uniform(key_of[1], (NSEQ, LEN, G * HD), jnp.float32, -1.0, 1.0) * shard_levels(key_of[1], (NSEQ, LEN, G * HD), ((0, 4), (1, 8)), -0.4, 0.0), -1.0, 1.0).astype(jnp.bfloat16)
    values = noise(key_of[2], (NSEQ, LEN, G * HD), 1.0, 6.0, ((0, 4), (1, 8)))
    attention_out = noise(key_of[3], (NSEQ, LEN, H * HD), 1.0, 6.0, ((0, 4), (1, 8)))
    grad_out = noise(key_of[4], (NSEQ, LEN, H * HD), 1.0, 6.0, ((0, 4), (1, 8)))
    layer_input = bell_draw_with(key_of[5], (NSEQ, LEN, DW), 1.0, 6.0, ((0, 4), (1, 8)), (1, 2, 8, 2.0))
    doc_lengths = jax.vmap(lambda own: ragged(own, NDOC, LEN, MOST, 2))(jax.random.split(key_of[6], NSEQ)).reshape((NSEQ, NDOC)).astype(jnp.int32)
    return dict(queries=queries, keys_rot=keys_rot, values=values, attention_out=attention_out, grad_out=grad_out, layer_input=layer_input, doc_lengths=doc_lengths)


def rope_back(grad_rows, places):
    count = grad_rows.shape[0]
    split = grad_rows.reshape(count, -1, HD)
    halfway = HD // 2
    inverse_freq = jnp.power(jnp.float32(1000000.0), -(jnp.arange(halfway, dtype=jnp.float32) * 2.0 / HD))
    angles = places.astype(jnp.float32)[:, None] * inverse_freq[None, :]
    cosine = jnp.cos(angles)[:, None, :]
    sine = jnp.sin(angles)[:, None, :]
    first = split[..., :halfway]
    second = split[..., halfway:]
    return jnp.concatenate([first * cosine + second * sine, second * cosine - first * sine], axis=-1).reshape(count, -1)

def reference(queries, keys_rot, values, attention_out, grad_out, layer_input, doc_lengths):
    softmax_scale = 1.0 / math.sqrt(HD)
    repeat = H // G
    block = min(512, LEN)
    nblocks = LEN // block
    window = MOST + block

    def one_sequence(operands):
        q_seq, k_seq, v_seq, o_seq, d_seq, lengths = operands
        starts = jnp.cumsum(lengths) - lengths
        places = jnp.arange(LEN, dtype=jnp.int32)
        doc_start = lax.optimization_barrier(jnp.max(jnp.where(starts[None, :] <= places[:, None], starts[None, :], 0), axis=1)).astype(jnp.int32)
        row_dots = lax.optimization_barrier(jnp.sum((o_seq.astype(jnp.float32) * d_seq.astype(jnp.float32)).reshape(LEN, G, repeat, HD), axis=-1))
        k_pad = jnp.concatenate([jnp.zeros((MOST, G * HD), jnp.bfloat16), k_seq], axis=0)
        v_pad = jnp.concatenate([jnp.zeros((MOST, G * HD), jnp.bfloat16), v_seq], axis=0)

        def step(carry, index):
            dk_pad, dv_pad = carry
            first = (index * block).astype(jnp.int32)
            query_block = lax.dynamic_slice_in_dim(q_seq, first, block, 0).astype(jnp.float32).reshape(block, G, repeat, HD)
            delta_block = lax.dynamic_slice_in_dim(d_seq, first, block, 0).astype(jnp.float32).reshape(block, G, repeat, HD)
            dots_blk = lax.dynamic_slice_in_dim(row_dots, first, block, 0)
            q_start = lax.dynamic_slice_in_dim(doc_start, first, block, 0)
            q_place = first + jnp.arange(block, dtype=jnp.int32)
            key_span_rows = lax.dynamic_slice_in_dim(k_pad, first, window, 0).astype(jnp.float32).reshape(window, G, HD)
            value_span_rows = lax.dynamic_slice_in_dim(v_pad, first, window, 0).astype(jnp.float32).reshape(window, G, HD)
            k_place = first - MOST + jnp.arange(window, dtype=jnp.int32)
            allowed = (k_place[None, :] >= q_start[:, None]) & (k_place[None, :] <= q_place[:, None])
            logit_matrix = jnp.einsum('qmju,bmu->mjqb', query_block, key_span_rows) * softmax_scale
            totals = lax.optimization_barrier(jnp.sum(jnp.where(allowed, jnp.exp(logit_matrix), 0.0), axis=-1))
            log_total = jnp.log(totals)
            probs = jnp.where(allowed, jnp.exp(logit_matrix - log_total[..., None]), 0.0)
            probability_narrow = probs.astype(jnp.bfloat16)
            probability_gradient = jnp.einsum('qmju,bmu->mjqb', delta_block, value_span_rows)
            dots_t = jnp.transpose(dots_blk, (1, 2, 0))
            logit_gradient = (probs * (probability_gradient - dots_t[..., None])).astype(jnp.bfloat16)
            value_grad_block = jnp.einsum('mfup,umfi->pmi', probability_narrow.astype(jnp.float32), delta_block)
            key_grad_block = jnp.einsum('mfup,umfi->pmi', logit_gradient.astype(jnp.float32), query_block) * softmax_scale
            query_grad_block = jnp.einsum('qvum,mqa->uqva', logit_gradient.astype(jnp.float32), key_span_rows) * softmax_scale
            dk_pad = lax.dynamic_update_slice_in_dim(dk_pad, lax.dynamic_slice_in_dim(dk_pad, first, window, 0) + key_grad_block.reshape(window, G * HD), first, 0)
            dv_pad = lax.dynamic_update_slice_in_dim(dv_pad, lax.dynamic_slice_in_dim(dv_pad, first, window, 0) + value_grad_block.reshape(window, G * HD), first, 0)
            return ((dk_pad, dv_pad), query_grad_block.reshape(block, H * HD))
        zeros_pad = jnp.zeros((MOST + LEN, G * HD), jnp.float32)
        (dk_pad, dv_pad), dq_blocks = lax.scan(step, (zeros_pad, zeros_pad), jnp.arange(nblocks, dtype=jnp.int32))
        local = places - doc_start
        grad_rot = dq_blocks.reshape(LEN, H * HD)
        grad_q = rope_back(grad_rot, local).astype(jnp.bfloat16)
        key_pre = rope_back(dk_pad[MOST:], local).astype(jnp.bfloat16)
        value_low = dv_pad[MOST:].astype(jnp.bfloat16)
        return (grad_q, key_pre, value_low)
    grad_query, key_all, value_all = lax.map(one_sequence, (queries, keys_rot, values, attention_out, grad_out, doc_lengths))
    inputs_flat = layer_input.reshape(-1, DW)
    grad_wk = jnp.dot(inputs_flat.T, key_all.reshape(-1, G * HD), preferred_element_type=jnp.float32)
    grad_wv = jnp.dot(inputs_flat.T, value_all.reshape(-1, G * HD), preferred_element_type=jnp.float32)
    return (grad_query, grad_wk, grad_wv)
```

```python
import math

import jax
import jax.numpy as jnp
from jax import lax
from jax.experimental import pallas as pl
from jax.experimental.pallas import tpu as pltpu
from jax.sharding import PartitionSpec as P

H = 20
G = 4
HD = 128
REP = H // G
DW = 2560
SPAN = 2
ROWS = 128
SCALE = 1.0 / math.sqrt(HD)
NT = (((1,), (1,)), ((), ()))


def passed_along(x, axis, by):
    peers = lax.axis_size(axis)
    pairs = [(i, i + by) for i in range(peers) if 0 <= i + by < peers]
    return lax.ppermute(x, axis, pairs)


def attention_kernel(
    start_ref, cos_ref, sin_ref, q_ref, o_ref, d_ref, k_ref, v_ref, near_ref, far_ref,
    dq_ref, own_ref, back1_ref, back2_ref,
    kwin, vwin, q_all, d_all, pt, dst, acc,
):
    step = pl.program_id(1)
    count = k_ref.shape[0]
    reach = SPAN * count
    window = reach + ROWS

    @pl.when(step == 0)
    def _():
        kwin[0:count] = far_ref[0]
        kwin[count : 2 * count] = near_ref[0]
        kwin[2 * count :] = k_ref[...]
        vwin[0:count] = far_ref[1]
        vwin[count : 2 * count] = near_ref[1]
        vwin[2 * count :] = v_ref[...]
        acc[...] = jnp.zeros_like(acc)

    first = pl.multiple_of(step * ROWS, ROWS)
    keys = kwin[pl.ds(first, window)]
    vals = vwin[pl.ds(first, window)]
    for j in range(REP):
        cols = slice(j * HD, (j + 1) * HD)
        rows = slice(j * ROWS, (j + 1) * ROWS)
        q_all[rows] = q_ref[:, cols]
        d_all[rows] = d_ref[:, cols]
    key_index = lax.broadcasted_iota(jnp.int32, (window, ROWS), 0)
    row_index = lax.broadcasted_iota(jnp.int32, (window, ROWS), 1)
    allowed = (key_index >= start_ref[...] - first) & (key_index <= row_index + reach)
    bias = jnp.where(allowed, 0.0, -1e30)
    scores = lax.dot_general(keys, q_all[...], NT, preferred_element_type=jnp.float32)
    gprobs = lax.dot_general(vals, d_all[...], NT, preferred_element_type=jnp.float32)
    for j in range(REP):
        cols = slice(j * HD, (j + 1) * HD)
        dots = jnp.sum(
            jnp.transpose(
                o_ref[:, cols].astype(jnp.float32) * d_ref[:, cols].astype(jnp.float32)
            ),
            axis=0,
            keepdims=True,
        )
        weights = jnp.exp2(scores[:, cols] * (SCALE * math.log2(math.e)) + bias)
        inverse = 1.0 / jnp.sum(weights, axis=0, keepdims=True)
        probs = weights * inverse
        pt[:, cols] = probs.astype(jnp.bfloat16)
        dst[:, cols] = (probs * (gprobs[:, cols] - dots)).astype(jnp.bfloat16)
    acc[1, pl.ds(first, window)] += jnp.dot(
        pt[...], d_all[...], preferred_element_type=jnp.float32
    )
    acc[0, pl.ds(first, window)] += jnp.dot(
        dst[...], q_all[...], preferred_element_type=jnp.float32
    )
    rot = jnp.dot(jnp.transpose(keys), dst[...], preferred_element_type=jnp.float32)
    half = HD // 2
    cosine = cos_ref[...] * SCALE
    sine = sin_ref[...] * SCALE
    for j in range(REP):
        cols = slice(j * HD, (j + 1) * HD)
        upper = rot[:half, cols]
        lower = rot[half:, cols]
        turned = jnp.concatenate(
            [upper * cosine + lower * sine, lower * cosine - upper * sine], axis=0
        )
        dq_ref[:, cols] = jnp.transpose(turned).astype(jnp.bfloat16)

    @pl.when(step == pl.num_programs(1) - 1)
    def _():
        for side, factor in ((0, SCALE), (1, 1.0)):
            back2_ref[side] = (acc[side, 0:count] * factor).astype(jnp.bfloat16)
            back1_ref[side] = (acc[side, count : 2 * count] * factor).astype(jnp.bfloat16)
            own_ref[side] = acc[side, 2 * count :] * factor


def attention(start, cos_t, sin_t, q, o, d, k, v, near, far):
    count = q.shape[0]
    steps = count // ROWS
    window = SPAN * count + ROWS
    half = HD // 2
    by_step = lambda g, i: (0, i)
    wide = pl.BlockSpec((ROWS, REP * HD), lambda g, i: (i, g))
    narrow = pl.BlockSpec((count, HD), lambda g, i: (0, g))
    pair = pl.BlockSpec((2, count, HD), lambda g, i: (0, 0, g))
    flops = G * steps * 5 * 2 * window * REP * ROWS * HD
    return pl.pallas_call(
        attention_kernel,
        grid=(G, steps),
        in_specs=[
            pl.BlockSpec((1, ROWS), by_step),
            pl.BlockSpec((half, ROWS), by_step),
            pl.BlockSpec((half, ROWS), by_step),
            wide, wide, wide, narrow, narrow, pair, pair,
        ],
        out_specs=[wide, pair, pair, pair],
        out_shape=[
            jax.ShapeDtypeStruct((count, H * HD), jnp.bfloat16),
            jax.ShapeDtypeStruct((2, count, G * HD), jnp.float32),
            jax.ShapeDtypeStruct((2, count, G * HD), jnp.bfloat16),
            jax.ShapeDtypeStruct((2, count, G * HD), jnp.bfloat16),
        ],
        scratch_shapes=[
            pltpu.VMEM(((SPAN + 1) * count, HD), jnp.bfloat16),
            pltpu.VMEM(((SPAN + 1) * count, HD), jnp.bfloat16),
            pltpu.VMEM((REP * ROWS, HD), jnp.bfloat16),
            pltpu.VMEM((REP * ROWS, HD), jnp.bfloat16),
            pltpu.VMEM((window, REP * ROWS), jnp.bfloat16),
            pltpu.VMEM((window, REP * ROWS), jnp.bfloat16),
            pltpu.VMEM((2, (SPAN + 1) * count, HD), jnp.float32),
        ],
        compiler_params=pltpu.CompilerParams(vmem_limit_bytes=48 << 20),
        cost_estimate=pl.CostEstimate(
            flops=2 * flops, bytes_accessed=16 << 20, transcendentals=steps * G * window * REP * ROWS
        ),
    )(start, cos_t, sin_t, q, o, d, k, v, near, far)


def on_device(queries, keys_rot, values, attention_out, grad_out, layer_input, doc_lengths):
    k_rows = keys_rot[0]
    v_rows = values[0]
    lengths = doc_lengths[0]
    count = k_rows.shape[0]
    shard = lax.axis_index("ctx")
    inputs = lax.all_gather(layer_input[0], "fsdp", axis=0, tiled=True)
    kv = jnp.stack([k_rows, v_rows])
    far = passed_along(kv, "ctx", 2)
    near = passed_along(kv, "ctx", 1)
    place = shard * count + jnp.arange(count, dtype=jnp.int32)
    starts = jnp.cumsum(lengths) - lengths
    start = jnp.max(jnp.where(starts[:, None] <= place[None, :], starts[:, None], 0), axis=0)
    local = (place - start).astype(jnp.float32)
    half = HD // 2
    inverse_freq = jnp.power(
        jnp.float32(1000000.0), -(jnp.arange(half, dtype=jnp.float32) * 2.0 / HD)
    )
    angles = inverse_freq[:, None] * local[None, :]
    cos_t = jnp.cos(angles)
    sin_t = jnp.sin(angles)
    relative = (start - (shard - SPAN) * count)[None, :]
    dq, own, back1, back2 = attention(
        relative, cos_t, sin_t, queries[0], attention_out[0], grad_out[0],
        k_rows, v_rows, near, far,
    )
    back2 = passed_along(back2, "ctx", -2)
    back1 = passed_along(back1, "ctx", -1)
    total = own + back1.astype(jnp.float32) + back2.astype(jnp.float32)
    heads = total[0].reshape(count, G, HD)
    cosine = cos_t.T[:, None, :]
    sine = sin_t.T[:, None, :]
    upper = heads[..., :half]
    lower = heads[..., half:]
    key_pre = jnp.concatenate(
        [upper * cosine + lower * sine, lower * cosine - upper * sine], axis=-1
    ).reshape(count, G * HD)
    both = jnp.stack([key_pre.astype(jnp.bfloat16), total[1].astype(jnp.bfloat16)])
    both = lax.all_to_all(both, "fsdp", split_axis=2, concat_axis=1, tiled=True)
    both = jnp.concatenate([both[0], both[1]], axis=1)
    term = lax.dot_general(
        inputs, both, (((0,), (0,)), ((), ())), preferred_element_type=jnp.float32
    )
    summed = lax.psum_scatter(term, "ctx", scatter_dimension=0, tiled=True)
    width = summed.shape[1] // 2
    return (dq[None], summed[:, :width], summed[:, width:])


def solution(mesh):
    in_specs = (
        P("fsdp", "ctx", None),
        P("fsdp", "ctx", None),
        P("fsdp", "ctx", None),
        P("fsdp", "ctx", None),
        P("fsdp", "ctx", None),
        P("fsdp", "ctx", None),
        P("fsdp", None),
    )
    out_specs = (P("fsdp", "ctx", None), P("ctx", "fsdp"), P("ctx", "fsdp"))
    return jax.shard_map(
        on_device, mesh=mesh, in_specs=in_specs, out_specs=out_specs, check_vma=False
    )
```

```python
import math

import jax
import jax.numpy as jnp
from jax import lax
from jax.experimental import pallas as pl
from jax.experimental.pallas import tpu as pltpu
from jax.sharding import PartitionSpec as P

H = 20
G = 4
HD = 128
REP = H // G
DW = 2560
SPAN = 2
ROWS = 128
SCALE = 1.0 / math.sqrt(HD)
NT = (((1,), (1,)), ((), ()))


def passed_along(x, axis, by):
    peers = lax.axis_size(axis)
    pairs = [(i, i + by) for i in range(peers) if 0 <= i + by < peers]
    return lax.ppermute(x, axis, pairs)


def attention_kernel(
    start_ref, cos_ref, sin_ref, q_ref, o_ref, d_ref, k_ref, v_ref, near_ref, far_ref,
    dq_ref, own_ref, back1_ref, back2_ref,
    kwin, vwin, q_all, d_all, pt, dst, acc,
):
    step = pl.program_id(1)
    count = k_ref.shape[0]
    reach = SPAN * count
    window = reach + ROWS

    @pl.when(step == 0)
    def _():
        kwin[0:count] = far_ref[0]
        kwin[count : 2 * count] = near_ref[0]
        kwin[2 * count :] = k_ref[...]
        vwin[0:count] = far_ref[1]
        vwin[count : 2 * count] = near_ref[1]
        vwin[2 * count :] = v_ref[...]
        acc[...] = jnp.zeros_like(acc)

    first = pl.multiple_of(step * ROWS, ROWS)
    keys = kwin[pl.ds(first, window)]
    vals = vwin[pl.ds(first, window)]
    for j in range(REP):
        cols = slice(j * HD, (j + 1) * HD)
        rows = slice(j * ROWS, (j + 1) * ROWS)
        q_all[rows] = q_ref[:, cols]
        d_all[rows] = d_ref[:, cols]
    key_index = lax.broadcasted_iota(jnp.int32, (window, ROWS), 0)
    row_index = lax.broadcasted_iota(jnp.int32, (window, ROWS), 1)
    allowed = (key_index >= start_ref[...] - first) & (key_index <= row_index + reach)
    bias = jnp.where(allowed, 0.0, -1e30)
    scores = lax.dot_general(keys, q_all[...], NT, preferred_element_type=jnp.float32)
    gprobs = lax.dot_general(vals, d_all[...], NT, preferred_element_type=jnp.float32)
    for j in range(REP):
        cols = slice(j * HD, (j + 1) * HD)
        dots = jnp.sum(
            jnp.transpose(
                o_ref[:, cols].astype(jnp.float32) * d_ref[:, cols].astype(jnp.float32)
            ),
            axis=0,
            keepdims=True,
        )
        weights = jnp.exp2(scores[:, cols] * (SCALE * math.log2(math.e)) + bias)
        inverse = 1.0 / jnp.sum(weights, axis=0, keepdims=True)
        probs = weights * inverse
        pt[:, cols] = probs.astype(jnp.bfloat16)
        dst[:, cols] = (probs * (gprobs[:, cols] - dots)).astype(jnp.bfloat16)
    acc[1, pl.ds(first, window)] += jnp.dot(
        pt[...], d_all[...], preferred_element_type=jnp.float32
    )
    acc[0, pl.ds(first, window)] += jnp.dot(
        dst[...], q_all[...], preferred_element_type=jnp.float32
    )
    rot = jnp.dot(jnp.transpose(keys), dst[...], preferred_element_type=jnp.float32)
    half = HD // 2
    cosine = cos_ref[...] * SCALE
    sine = sin_ref[...] * SCALE
    for j in range(REP):
        cols = slice(j * HD, (j + 1) * HD)
        upper = rot[:half, cols]
        lower = rot[half:, cols]
        turned = jnp.concatenate(
            [upper * cosine + lower * sine, lower * cosine - upper * sine], axis=0
        )
        dq_ref[:, cols] = jnp.transpose(turned).astype(jnp.bfloat16)

    @pl.when(step == pl.num_programs(1) - 1)
    def _():
        for side, factor in ((0, SCALE), (1, 1.0)):
            back2_ref[side] = (acc[side, 0:count] * factor).astype(jnp.bfloat16)
            back1_ref[side] = (acc[side, count : 2 * count] * factor).astype(jnp.bfloat16)
            own_ref[side] = acc[side, 2 * count :] * factor


def attention(start, cos_t, sin_t, q, o, d, k, v, near, far):
    count = q.shape[0]
    steps = count // ROWS
    window = SPAN * count + ROWS
    half = HD // 2
    by_step = lambda g, i: (0, i)
    wide = pl.BlockSpec((ROWS, REP * HD), lambda g, i: (i, g))
    narrow = pl.BlockSpec((count, HD), lambda g, i: (0, g))
    pair = pl.BlockSpec((2, count, HD), lambda g, i: (0, 0, g))
    flops = G * steps * 5 * 2 * window * REP * ROWS * HD
    return pl.pallas_call(
        attention_kernel,
        grid=(G, steps),
        in_specs=[
            pl.BlockSpec((1, ROWS), by_step),
            pl.BlockSpec((half, ROWS), by_step),
            pl.BlockSpec((half, ROWS), by_step),
            wide, wide, wide, narrow, narrow, pair, pair,
        ],
        out_specs=[wide, pair, pair, pair],
        out_shape=[
            jax.ShapeDtypeStruct((count, H * HD), jnp.bfloat16),
            jax.ShapeDtypeStruct((2, count, G * HD), jnp.float32),
            jax.ShapeDtypeStruct((2, count, G * HD), jnp.bfloat16),
            jax.ShapeDtypeStruct((2, count, G * HD), jnp.bfloat16),
        ],
        scratch_shapes=[
            pltpu.VMEM(((SPAN + 1) * count, HD), jnp.bfloat16),
            pltpu.VMEM(((SPAN + 1) * count, HD), jnp.bfloat16),
            pltpu.VMEM((REP * ROWS, HD), jnp.bfloat16),
            pltpu.VMEM((REP * ROWS, HD), jnp.bfloat16),
            pltpu.VMEM((window, REP * ROWS), jnp.bfloat16),
            pltpu.VMEM((window, REP * ROWS), jnp.bfloat16),
            pltpu.VMEM((2, (SPAN + 1) * count, HD), jnp.float32),
        ],
        compiler_params=pltpu.CompilerParams(vmem_limit_bytes=48 << 20),
        cost_estimate=pl.CostEstimate(
            flops=2 * flops, bytes_accessed=16 << 20, transcendentals=steps * G * window * REP * ROWS
        ),
    )(start, cos_t, sin_t, q, o, d, k, v, near, far)


def reduce_kernel(
    term_ref, out_ref, paired, mine, got, send_one, recv_one, send_two, recv_two
):
    peers = term_ref.shape[0]
    half = peers // 2
    me = lax.axis_index("ctx")
    parity = lax.rem(me, 2)
    spot = lax.div(me, 2)
    pair = me + 1 - 2 * parity
    barrier = pltpu.get_barrier_semaphore()
    pl.semaphore_signal(
        barrier, inc=1, device_id={"ctx": pair}, device_id_type=pl.DeviceIdType.MESH
    )
    for k in range(half - 1):
        other = 2 * lax.rem(spot + k + 1, half) + parity
        pl.semaphore_signal(
            barrier, inc=1, device_id={"ctx": other}, device_id_type=pl.DeviceIdType.MESH
        )
    pl.semaphore_wait(barrier, half)
    firsts = []
    for k in range(half):
        target = lax.rem(spot + k + 1, half)
        copy = pltpu.make_async_remote_copy(
            src_ref=term_ref.at[2 * target + 1 - parity],
            dst_ref=paired.at[k],
            send_sem=send_one.at[k],
            recv_sem=recv_one.at[k],
            device_id={"ctx": pair},
            device_id_type=pl.DeviceIdType.MESH,
        )
        copy.start()
        firsts.append(copy)
    seconds = []
    total = None
    for k in range(half):
        target = lax.rem(spot + k + 1, half)
        firsts[k].wait_recv()
        summed = term_ref[2 * target + parity].astype(jnp.float32) + paired[k].astype(
            jnp.float32
        )
        if k == half - 1:
            out_ref[...] = summed
            break
        mine[k] = summed.astype(jnp.bfloat16)
        copy = pltpu.make_async_remote_copy(
            src_ref=mine.at[k],
            dst_ref=got.at[k],
            send_sem=send_two.at[k],
            recv_sem=recv_two.at[k],
            device_id={"ctx": 2 * target + parity},
            device_id_type=pl.DeviceIdType.MESH,
        )
        copy.start()
        seconds.append(copy)
    for copy in seconds:
        copy.wait_recv()
    total = out_ref[...]
    for k in range(half - 1):
        total = total + got[k].astype(jnp.float32)
    out_ref[...] = total
    for copy in firsts + seconds:
        copy.wait_send()


def reduced(term, peers):
    rows, width = term.shape[0] // peers, term.shape[1]
    half = peers // 2
    whole = pl.BlockSpec(memory_space=pltpu.VMEM)
    return pl.pallas_call(
        reduce_kernel,
        in_specs=[whole],
        out_specs=whole,
        out_shape=jax.ShapeDtypeStruct((rows, width), jnp.float32),
        scratch_shapes=[
            pltpu.VMEM((half, rows, width), jnp.bfloat16),
            pltpu.VMEM((half - 1, rows, width), jnp.bfloat16),
            pltpu.VMEM((half - 1, rows, width), jnp.bfloat16),
            pltpu.SemaphoreType.DMA((half,)),
            pltpu.SemaphoreType.DMA((half,)),
            pltpu.SemaphoreType.DMA((half - 1,)),
            pltpu.SemaphoreType.DMA((half - 1,)),
        ],
        compiler_params=pltpu.CompilerParams(collective_id=1, has_side_effects=True),
    )(term.reshape(peers, rows, width))


def on_device(queries, keys_rot, values, attention_out, grad_out, layer_input, doc_lengths):
    k_rows = keys_rot[0]
    v_rows = values[0]
    lengths = doc_lengths[0]
    count = k_rows.shape[0]
    shard = lax.axis_index("ctx")
    inputs = lax.all_gather(layer_input[0], "fsdp", axis=0, tiled=True)
    kv = jnp.stack([k_rows, v_rows])
    far = passed_along(kv, "ctx", 2)
    near = passed_along(kv, "ctx", 1)
    place = shard * count + jnp.arange(count, dtype=jnp.int32)
    starts = jnp.cumsum(lengths) - lengths
    start = jnp.max(jnp.where(starts[:, None] <= place[None, :], starts[:, None], 0), axis=0)
    local = (place - start).astype(jnp.float32)
    half = HD // 2
    inverse_freq = jnp.power(
        jnp.float32(1000000.0), -(jnp.arange(half, dtype=jnp.float32) * 2.0 / HD)
    )
    angles = inverse_freq[:, None] * local[None, :]
    cos_t = jnp.cos(angles)
    sin_t = jnp.sin(angles)
    relative = (start - (shard - SPAN) * count)[None, :]
    dq, own, back1, back2 = attention(
        relative, cos_t, sin_t, queries[0], attention_out[0], grad_out[0],
        k_rows, v_rows, near, far,
    )
    back2 = passed_along(back2, "ctx", -2)
    back1 = passed_along(back1, "ctx", -1)
    total = own + back1.astype(jnp.float32) + back2.astype(jnp.float32)
    heads = total[0].reshape(count, G, HD)
    cosine = cos_t.T[:, None, :]
    sine = sin_t.T[:, None, :]
    upper = heads[..., :half]
    lower = heads[..., half:]
    key_pre = jnp.concatenate(
        [upper * cosine + lower * sine, lower * cosine - upper * sine], axis=-1
    ).reshape(count, G * HD)
    both = jnp.stack([key_pre.astype(jnp.bfloat16), total[1].astype(jnp.bfloat16)])
    both = lax.all_to_all(both, "fsdp", split_axis=2, concat_axis=1, tiled=True)
    both = jnp.concatenate([both[0], both[1]], axis=1)
    term = lax.dot_general(
        inputs, both, (((0,), (0,)), ((), ())), preferred_element_type=jnp.float32
    )
    summed = reduced(term.astype(jnp.bfloat16), lax.axis_size("ctx"))
    width = summed.shape[1] // 2
    return (dq[None], summed[:, :width], summed[:, width:])


def solution(mesh):
    in_specs = (
        P("fsdp", "ctx", None),
        P("fsdp", "ctx", None),
        P("fsdp", "ctx", None),
        P("fsdp", "ctx", None),
        P("fsdp", "ctx", None),
        P("fsdp", "ctx", None),
        P("fsdp", None),
    )
    out_specs = (P("fsdp", "ctx", None), P("ctx", "fsdp"), P("ctx", "fsdp"))
    return jax.shard_map(
        on_device, mesh=mesh, in_specs=in_specs, out_specs=out_specs, check_vma=False
    )
```

```python
import math

import jax
import jax.numpy as jnp
from jax import lax
from jax.experimental import pallas as pl
from jax.experimental.pallas import tpu as pltpu
from jax.sharding import PartitionSpec as P

H = 20
G = 4
HD = 128
REP = H // G
DW = 2560
SPAN = 2
ROWS = 128
SCALE = 1.0 / math.sqrt(HD)
NT = (((1,), (1,)), ((), ()))


def attention_kernel(
    start_ref, cos_ref, sin_ref, key_cos_ref, key_sin_ref, q_ref, o_ref, d_ref, k_ref, v_ref,
    dq_ref, both_ref,
    kwin, vwin, q_all, d_all, pt, dst, acc,
    own_kv, far_kv, near_kv, pair_out, pair_in, back_out, back_in, own_acc, done_out, done_in,
    far_sems, near_sems, pair_sems, back_sems, done_sems,
):
    group = pl.program_id(0)
    step = pl.program_id(1)
    count = k_ref.shape[0]
    reach = SPAN * count
    window = reach + ROWS
    peers = lax.axis_size("ctx")
    seqs = lax.axis_size("fsdp")
    me = lax.axis_index("ctx")
    seq = lax.axis_index("fsdp")
    odd = lax.rem(me, 2) == 1
    even = lax.rem(me, 2) == 0
    pair = me + 1 - 2 * lax.rem(me, 2)
    has_before = me >= 2
    has_after = me < peers - 2
    first_step = step == 0
    last_step = step == pl.num_programs(1) - 1

    def remote(src, dst_buf, sems, index, where):
        return pltpu.make_async_remote_copy(
            src_ref=src,
            dst_ref=dst_buf,
            send_sem=sems.at[0, index],
            recv_sem=sems.at[1, index],
            device_id=where,
            device_id_type=pl.DeviceIdType.MESH,
        )

    def far_copy(g):
        return remote(own_kv.at[g], far_kv.at[g], far_sems, g, {"ctx": me + 2})

    def near_own(g):
        return remote(own_kv.at[g], near_kv.at[g], near_sems, g, {"ctx": pair})

    def near_relay(g):
        return remote(far_kv.at[g], near_kv.at[g], near_sems, g, {"ctx": pair})

    def pair_copy(g):
        return remote(pair_out.at[g], pair_in.at[g], pair_sems, g, {"ctx": pair})

    def back_copy(g):
        return remote(back_out.at[g], back_in.at[g], back_sems, g, {"ctx": me - 2})

    def done_copy(g):
        return pltpu.make_async_remote_copy(
            src_ref=done_out.at[g],
            dst_ref=done_in.at[seq],
            send_sem=done_sems.at[0, g],
            recv_sem=done_sems.at[1, seq],
            device_id={"fsdp": g},
            device_id_type=pl.DeviceIdType.MESH,
        )

    def done_arrival(f):
        return pltpu.make_async_remote_copy(
            src_ref=done_out.at[f],
            dst_ref=done_in.at[f],
            send_sem=done_sems.at[0, f],
            recv_sem=done_sems.at[1, f],
            device_id={"fsdp": f},
            device_id_type=pl.DeviceIdType.MESH,
        )

    def relay_near(g):
        far_copy(g).wait_recv()
        near_relay(g).start()

    def relay_back(g):
        pair_copy(g).wait_recv()
        back_out[g] = (
            back_out[g].astype(jnp.float32) + pair_in[g].astype(jnp.float32)
        ).astype(jnp.bfloat16)
        back_copy(g).start()

    def finish(g):
        @pl.when(even)
        def _():
            pair_copy(g).wait_recv()
            own_acc[g] += pair_in[g].astype(jnp.float32)

        @pl.when(has_after)
        def _():
            back_copy(g).wait_recv()
            own_acc[g] += back_in[g].astype(jnp.float32)

        keyed = own_acc[g, 0]
        turned = keyed * key_cos_ref[...] + pltpu.roll(keyed, HD // 2, 1) * key_sin_ref[...]
        done_out[g, 0] = turned.astype(jnp.bfloat16)
        done_out[g, 1] = own_acc[g, 1].astype(jnp.bfloat16)

        @pl.when(seq != g)
        def _():
            done_copy(g).start()

    @pl.when(first_step & (group == 0))
    def _():
        barrier = pltpu.get_barrier_semaphore()

        def greet(where):
            pl.semaphore_signal(
                barrier, inc=1, device_id=where, device_id_type=pl.DeviceIdType.MESH
            )

        greet({"ctx": pair})
        for k in range(1, seqs):
            greet({"fsdp": lax.rem(seq + k, seqs)})

        @pl.when(has_after)
        def _():
            greet({"ctx": me + 2})

        @pl.when(has_before)
        def _():
            greet({"ctx": me - 2})

        for g in range(G):
            own_kv[g, 0] = k_ref[:, g * HD : (g + 1) * HD]
            own_kv[g, 1] = v_ref[:, g * HD : (g + 1) * HD]
        @pl.when(has_after & has_before)
        def _():
            pl.semaphore_wait(barrier, seqs + 2)

        @pl.when(jnp.logical_not(has_after & has_before))
        def _():
            pl.semaphore_wait(barrier, seqs + 1)

        for g in range(G):

            @pl.when(has_after)
            def _():
                far_copy(g).start()

            @pl.when(even)
            def _():
                near_own(g).start()

        @pl.when(odd & has_before)
        def _():
            relay_near(0)

    @pl.when(first_step & odd & has_before & (group < G - 1))
    def _():
        relay_near(group + 1)

    @pl.when(first_step)
    def _():
        kwin[2 * count :] = own_kv[group, 0]
        vwin[2 * count :] = own_kv[group, 1]
        acc[...] = jnp.zeros_like(acc)

        @pl.when(even & has_before)
        def _():
            far_copy(group).wait_recv()

        @pl.when(has_before)
        def _():
            kwin[0:count] = far_kv[group, 0]
            vwin[0:count] = far_kv[group, 1]

        @pl.when(me < 2)
        def _():
            kwin[0:count] = jnp.zeros((count, HD), jnp.bfloat16)
            vwin[0:count] = jnp.zeros((count, HD), jnp.bfloat16)

        @pl.when(me >= 1)
        def _():
            near_own(group).wait_recv()
            kwin[count : 2 * count] = near_kv[group, 0]
            vwin[count : 2 * count] = near_kv[group, 1]

        @pl.when(me < 1)
        def _():
            kwin[count : 2 * count] = jnp.zeros((count, HD), jnp.bfloat16)
            vwin[count : 2 * count] = jnp.zeros((count, HD), jnp.bfloat16)

    first = pl.multiple_of(step * ROWS, ROWS)
    keys = kwin[pl.ds(first, window)]
    vals = vwin[pl.ds(first, window)]
    for j in range(REP):
        cols = slice(j * HD, (j + 1) * HD)
        rows = slice(j * ROWS, (j + 1) * ROWS)
        q_all[rows] = q_ref[:, cols]
        d_all[rows] = d_ref[:, cols]
    key_index = lax.broadcasted_iota(jnp.int32, (window, ROWS), 0)
    row_index = lax.broadcasted_iota(jnp.int32, (window, ROWS), 1)
    allowed = (key_index >= start_ref[...] - first) & (key_index <= row_index + reach)
    bias = jnp.where(allowed, 0.0, -1e30)
    scores = lax.dot_general(keys, q_all[...], NT, preferred_element_type=jnp.float32)
    gprobs = lax.dot_general(vals, d_all[...], NT, preferred_element_type=jnp.float32)
    for j in range(REP):
        cols = slice(j * HD, (j + 1) * HD)
        dots = jnp.sum(
            jnp.transpose(
                o_ref[:, cols].astype(jnp.float32) * d_ref[:, cols].astype(jnp.float32)
            ),
            axis=0,
            keepdims=True,
        )
        weights = jnp.exp2(scores[:, cols] * (SCALE * math.log2(math.e)) + bias)
        inverse = 1.0 / jnp.sum(weights, axis=0, keepdims=True)
        probs = weights * inverse
        pt[:, cols] = probs.astype(jnp.bfloat16)
        dst[:, cols] = (probs * (gprobs[:, cols] - dots)).astype(jnp.bfloat16)
    acc[1, pl.ds(first, window)] += jnp.dot(
        pt[...], d_all[...], preferred_element_type=jnp.float32
    )
    acc[0, pl.ds(first, window)] += jnp.dot(
        dst[...], q_all[...], preferred_element_type=jnp.float32
    )
    rot = jnp.dot(jnp.transpose(keys), dst[...], preferred_element_type=jnp.float32)
    half = HD // 2
    cosine = cos_ref[...] * SCALE
    sine = sin_ref[...] * SCALE
    for j in range(REP):
        cols = slice(j * HD, (j + 1) * HD)
        upper = rot[:half, cols]
        lower = rot[half:, cols]
        turned = jnp.concatenate(
            [upper * cosine + lower * sine, lower * cosine - upper * sine], axis=0
        )
        dq_ref[:, cols] = jnp.transpose(turned).astype(jnp.bfloat16)

    @pl.when(last_step)
    def _():
        for side, factor in ((0, SCALE), (1, 1.0)):
            pair_out[group, side] = (acc[side, count : 2 * count] * factor).astype(jnp.bfloat16)
            back_out[group, side] = (acc[side, 0:count] * factor).astype(jnp.bfloat16)
            own_acc[group, side] = acc[side, 2 * count :] * factor

        @pl.when(me >= 1)
        def _():
            pair_copy(group).start()

        @pl.when(even & has_before)
        def _():
            back_copy(group).start()

        @pl.when(odd & has_before & (group >= 1))
        def _():
            relay_back(group - 1)

        @pl.when(group >= 2)
        def _():
            finish(group - 2)

    @pl.when(last_step & (group == G - 1))
    def _():
        @pl.when(odd & has_before)
        def _():
            relay_back(G - 1)

        finish(G - 2)
        finish(G - 1)

        for f in range(seqs):
            rows = slice(f * count, (f + 1) * count)

            @pl.when(seq == f)
            def _():
                both_ref[rows, 0:HD] = done_out[f, 0]
                both_ref[rows, HD:] = done_out[f, 1]

            @pl.when(seq != f)
            def _():
                done_arrival(f).wait_recv()
                both_ref[rows, 0:HD] = done_in[f, 0]
                both_ref[rows, HD:] = done_in[f, 1]
                done_arrival(f).wait_send()

        for g in range(G):

            @pl.when(has_after)
            def _():
                far_copy(g).wait_send()

            @pl.when(even | has_before)
            def _():
                near_own(g).wait_send()

            @pl.when(me >= 1)
            def _():
                pair_copy(g).wait_send()

            @pl.when(has_before)
            def _():
                back_copy(g).wait_send()


def attention(start, cos_t, sin_t, key_cos, key_sin, q, o, d, k, v, seqs):
    count = q.shape[0]
    steps = count // ROWS
    window = SPAN * count + ROWS
    half = HD // 2
    by_step = lambda g, i: (0, i)
    fixed = lambda g, i: (0, 0)
    wide = pl.BlockSpec((ROWS, REP * HD), lambda g, i: (i, g))
    rows = pl.BlockSpec((count, G * HD), fixed)
    table = pl.BlockSpec((count, HD), fixed)
    flops = G * steps * 5 * 2 * window * REP * ROWS * HD
    slots = pltpu.VMEM((G, 2, count, HD), jnp.bfloat16)
    sems = pltpu.SemaphoreType.DMA((2, G))
    assert seqs == G
    return pl.pallas_call(
        attention_kernel,
        grid=(G, steps),
        in_specs=[
            pl.BlockSpec((1, ROWS), by_step),
            pl.BlockSpec((half, ROWS), by_step),
            pl.BlockSpec((half, ROWS), by_step),
            table, table, wide, wide, wide, rows, rows,
        ],
        out_specs=[wide, pl.BlockSpec((seqs * count, 2 * HD), fixed)],
        out_shape=[
            jax.ShapeDtypeStruct((count, H * HD), jnp.bfloat16),
            jax.ShapeDtypeStruct((seqs * count, 2 * HD), jnp.bfloat16),
        ],
        scratch_shapes=[
            pltpu.VMEM(((SPAN + 1) * count, HD), jnp.bfloat16),
            pltpu.VMEM(((SPAN + 1) * count, HD), jnp.bfloat16),
            pltpu.VMEM((REP * ROWS, HD), jnp.bfloat16),
            pltpu.VMEM((REP * ROWS, HD), jnp.bfloat16),
            pltpu.VMEM((window, REP * ROWS), jnp.bfloat16),
            pltpu.VMEM((window, REP * ROWS), jnp.bfloat16),
            pltpu.VMEM((2, (SPAN + 1) * count, HD), jnp.float32),
            slots, slots, slots, slots, slots, slots, slots,
            pltpu.VMEM((G, 2, count, HD), jnp.float32),
            slots, slots,
            sems, sems, sems, sems, sems,
        ],
        compiler_params=pltpu.CompilerParams(
            vmem_limit_bytes=48 << 20, collective_id=0, has_side_effects=True
        ),
        cost_estimate=pl.CostEstimate(
            flops=2 * flops, bytes_accessed=16 << 20, transcendentals=steps * G * window * REP * ROWS
        ),
    )(start, cos_t, sin_t, key_cos, key_sin, q, o, d, k, v)


def reduce_kernel(
    term_ref, out_ref, paired, mine, got, send_one, recv_one, send_two, recv_two
):
    peers = term_ref.shape[0]
    half = peers // 2
    me = lax.axis_index("ctx")
    parity = lax.rem(me, 2)
    spot = lax.div(me, 2)
    pair = me + 1 - 2 * parity
    barrier = pltpu.get_barrier_semaphore()
    pl.semaphore_signal(
        barrier, inc=1, device_id={"ctx": pair}, device_id_type=pl.DeviceIdType.MESH
    )
    for k in range(half - 1):
        other = 2 * lax.rem(spot + k + 1, half) + parity
        pl.semaphore_signal(
            barrier, inc=1, device_id={"ctx": other}, device_id_type=pl.DeviceIdType.MESH
        )
    pl.semaphore_wait(barrier, half)
    firsts = []
    for k in range(half):
        target = lax.rem(spot + k + 1, half)
        copy = pltpu.make_async_remote_copy(
            src_ref=term_ref.at[2 * target + 1 - parity],
            dst_ref=paired.at[k],
            send_sem=send_one.at[k],
            recv_sem=recv_one.at[k],
            device_id={"ctx": pair},
            device_id_type=pl.DeviceIdType.MESH,
        )
        copy.start()
        firsts.append(copy)
    seconds = []
    total = None
    for k in range(half):
        target = lax.rem(spot + k + 1, half)
        firsts[k].wait_recv()
        summed = term_ref[2 * target + parity].astype(jnp.float32) + paired[k].astype(
            jnp.float32
        )
        if k == half - 1:
            out_ref[...] = summed
            break
        mine[k] = summed.astype(jnp.bfloat16)
        copy = pltpu.make_async_remote_copy(
            src_ref=mine.at[k],
            dst_ref=got.at[k],
            send_sem=send_two.at[k],
            recv_sem=recv_two.at[k],
            device_id={"ctx": 2 * target + parity},
            device_id_type=pl.DeviceIdType.MESH,
        )
        copy.start()
        seconds.append(copy)
    for copy in seconds:
        copy.wait_recv()
    total = out_ref[...]
    for k in range(half - 1):
        total = total + got[k].astype(jnp.float32)
    out_ref[...] = total
    for copy in firsts + seconds:
        copy.wait_send()


def reduced(term, peers):
    rows, width = term.shape[0] // peers, term.shape[1]
    half = peers // 2
    whole = pl.BlockSpec(memory_space=pltpu.VMEM)
    return pl.pallas_call(
        reduce_kernel,
        in_specs=[whole],
        out_specs=whole,
        out_shape=jax.ShapeDtypeStruct((rows, width), jnp.float32),
        scratch_shapes=[
            pltpu.VMEM((half, rows, width), jnp.bfloat16),
            pltpu.VMEM((half - 1, rows, width), jnp.bfloat16),
            pltpu.VMEM((half - 1, rows, width), jnp.bfloat16),
            pltpu.SemaphoreType.DMA((half,)),
            pltpu.SemaphoreType.DMA((half,)),
            pltpu.SemaphoreType.DMA((half - 1,)),
            pltpu.SemaphoreType.DMA((half - 1,)),
        ],
        compiler_params=pltpu.CompilerParams(collective_id=1, has_side_effects=True),
    )(term.reshape(peers, rows, width))


def on_device(queries, keys_rot, values, attention_out, grad_out, layer_input, doc_lengths):
    k_rows = keys_rot[0]
    v_rows = values[0]
    lengths = doc_lengths[0]
    count = k_rows.shape[0]
    shard = lax.axis_index("ctx")
    inputs = lax.all_gather(layer_input[0], "fsdp", axis=0, tiled=True)
    place = shard * count + jnp.arange(count, dtype=jnp.int32)
    starts = jnp.cumsum(lengths) - lengths
    start = jnp.max(jnp.where(starts[:, None] <= place[None, :], starts[:, None], 0), axis=0)
    local = (place - start).astype(jnp.float32)
    half = HD // 2
    inverse_freq = jnp.power(
        jnp.float32(1000000.0), -(jnp.arange(half, dtype=jnp.float32) * 2.0 / HD)
    )
    angles = inverse_freq[:, None] * local[None, :]
    cos_t = jnp.cos(angles)
    sin_t = jnp.sin(angles)
    relative = (start - (shard - SPAN) * count)[None, :]
    key_cos = jnp.concatenate([cos_t.T, cos_t.T], axis=1)
    key_sin = jnp.concatenate([sin_t.T, -sin_t.T], axis=1)
    dq, both = attention(
        relative, cos_t, sin_t, key_cos, key_sin, queries[0], attention_out[0], grad_out[0],
        k_rows, v_rows, lax.axis_size("fsdp"),
    )
    term = lax.dot_general(
        inputs, both, (((0,), (0,)), ((), ())), preferred_element_type=jnp.float32
    )
    summed = reduced(term.astype(jnp.bfloat16), lax.axis_size("ctx"))
    width = summed.shape[1] // 2
    return (dq[None], summed[:, :width], summed[:, width:])


def solution(mesh):
    in_specs = (
        P("fsdp", "ctx", None),
        P("fsdp", "ctx", None),
        P("fsdp", "ctx", None),
        P("fsdp", "ctx", None),
        P("fsdp", "ctx", None),
        P("fsdp", "ctx", None),
        P("fsdp", None),
    )
    out_specs = (P("fsdp", "ctx", None), P("ctx", "fsdp"), P("ctx", "fsdp"))
    return jax.shard_map(
        on_device, mesh=mesh, in_specs=in_specs, out_specs=out_specs, check_vma=False
    )
```

```python
import math

import jax
import jax.numpy as jnp
from jax import lax
from jax.experimental import pallas as pl
from jax.experimental.pallas import tpu as pltpu
from jax.sharding import PartitionSpec as P

H = 20
G = 4
HD = 128
REP = H // G
DW = 2560
SPAN = 2
ROWS = 128
SCALE = 1.0 / math.sqrt(HD)
NT = (((1,), (1,)), ((), ()))


def attention_kernel(
    start_ref, cos_ref, sin_ref, key_cos_ref, key_sin_ref, q_ref, o_ref, d_ref, k_ref, v_ref,
    dq_ref, both_ref,
    kwin, vwin, q_all, d_all, pt, dst, acc,
    own_kv, far_kv, near_kv, pair_out, pair_in, back_out, back_in, own_acc, done_out, done_in,
    far_sems, near_sems, pair_sems, back_sems, done_sems,
):
    group = pl.program_id(0)
    step = pl.program_id(1)
    count = k_ref.shape[0]
    reach = SPAN * count
    window = reach + ROWS
    peers = lax.axis_size("ctx")
    seqs = lax.axis_size("fsdp")
    me = lax.axis_index("ctx")
    seq = lax.axis_index("fsdp")
    odd = lax.rem(me, 2) == 1
    even = lax.rem(me, 2) == 0
    pair = me + 1 - 2 * lax.rem(me, 2)
    has_before = me >= 2
    has_after = me < peers - 2
    first_step = step == 0
    last_step = step == pl.num_programs(1) - 1

    def remote(src, dst_buf, sems, index, where):
        return pltpu.make_async_remote_copy(
            src_ref=src,
            dst_ref=dst_buf,
            send_sem=sems.at[0, index],
            recv_sem=sems.at[1, index],
            device_id=where,
            device_id_type=pl.DeviceIdType.MESH,
        )

    def far_copy(g):
        return remote(own_kv.at[g], far_kv.at[g], far_sems, g, {"ctx": me + 2})

    def near_own(g):
        return remote(own_kv.at[g], near_kv.at[g], near_sems, g, {"ctx": pair})

    def near_relay(g):
        return remote(far_kv.at[g], near_kv.at[g], near_sems, g, {"ctx": pair})

    def pair_copy(g):
        return remote(pair_out.at[g], pair_in.at[g], pair_sems, g, {"ctx": pair})

    def back_copy(g):
        return remote(back_out.at[g], back_in.at[g], back_sems, g, {"ctx": me - 2})

    def done_copy(g):
        return pltpu.make_async_remote_copy(
            src_ref=done_out.at[g],
            dst_ref=done_in.at[seq],
            send_sem=done_sems.at[0, g],
            recv_sem=done_sems.at[1, seq],
            device_id={"fsdp": g},
            device_id_type=pl.DeviceIdType.MESH,
        )

    def done_arrival(f):
        return pltpu.make_async_remote_copy(
            src_ref=done_out.at[f],
            dst_ref=done_in.at[f],
            send_sem=done_sems.at[0, f],
            recv_sem=done_sems.at[1, f],
            device_id={"fsdp": f},
            device_id_type=pl.DeviceIdType.MESH,
        )

    def relay_near(g):
        far_copy(g).wait_recv()
        near_relay(g).start()

    def relay_back(g):
        pair_copy(g).wait_recv()
        back_out[g] = (
            back_out[g].astype(jnp.float32) + pair_in[g].astype(jnp.float32)
        ).astype(jnp.bfloat16)
        back_copy(g).start()

    def finish(g):
        @pl.when(even)
        def _():
            pair_copy(g).wait_recv()
            own_acc[g] += pair_in[g].astype(jnp.float32)

        @pl.when(has_after)
        def _():
            back_copy(g).wait_recv()
            own_acc[g] += back_in[g].astype(jnp.float32)

        keyed = own_acc[g, 0]
        turned = keyed * key_cos_ref[...] + pltpu.roll(keyed, HD // 2, 1) * key_sin_ref[...]
        done_out[g, 0] = turned.astype(jnp.bfloat16)
        done_out[g, 1] = own_acc[g, 1].astype(jnp.bfloat16)

        @pl.when(seq != g)
        def _():
            done_copy(g).start()

    @pl.when(first_step & (group == 0))
    def _():
        barrier = pltpu.get_barrier_semaphore()

        def greet(where):
            pl.semaphore_signal(
                barrier, inc=1, device_id=where, device_id_type=pl.DeviceIdType.MESH
            )

        greet({"ctx": pair})
        for k in range(1, seqs):
            greet({"fsdp": lax.rem(seq + k, seqs)})

        @pl.when(has_after)
        def _():
            greet({"ctx": me + 2})

        @pl.when(has_before)
        def _():
            greet({"ctx": me - 2})

        for g in range(G):
            own_kv[g, 0] = k_ref[:, g * HD : (g + 1) * HD]
            own_kv[g, 1] = v_ref[:, g * HD : (g + 1) * HD]
        @pl.when(has_after & has_before)
        def _():
            pl.semaphore_wait(barrier, seqs + 2)

        @pl.when(jnp.logical_not(has_after & has_before))
        def _():
            pl.semaphore_wait(barrier, seqs + 1)

        for g in range(G):

            @pl.when(has_after)
            def _():
                far_copy(g).start()

            @pl.when(even)
            def _():
                near_own(g).start()

        @pl.when(odd & has_before)
        def _():
            relay_near(0)

    @pl.when(first_step & odd & has_before & (group < G - 1))
    def _():
        relay_near(group + 1)

    @pl.when(first_step)
    def _():
        kwin[2 * count :] = own_kv[group, 0]
        vwin[2 * count :] = own_kv[group, 1]
        acc[...] = jnp.zeros_like(acc)

        @pl.when(even & has_before)
        def _():
            far_copy(group).wait_recv()

        @pl.when(has_before)
        def _():
            kwin[0:count] = far_kv[group, 0]
            vwin[0:count] = far_kv[group, 1]

        @pl.when(me < 2)
        def _():
            kwin[0:count] = jnp.zeros((count, HD), jnp.bfloat16)
            vwin[0:count] = jnp.zeros((count, HD), jnp.bfloat16)

        @pl.when(me >= 1)
        def _():
            near_own(group).wait_recv()
            kwin[count : 2 * count] = near_kv[group, 0]
            vwin[count : 2 * count] = near_kv[group, 1]

        @pl.when(me < 1)
        def _():
            kwin[count : 2 * count] = jnp.zeros((count, HD), jnp.bfloat16)
            vwin[count : 2 * count] = jnp.zeros((count, HD), jnp.bfloat16)

    first = pl.multiple_of(step * ROWS, ROWS)
    keys = kwin[pl.ds(first, window)]
    vals = vwin[pl.ds(first, window)]
    for j in range(REP):
        cols = slice(j * HD, (j + 1) * HD)
        rows = slice(j * ROWS, (j + 1) * ROWS)
        q_all[rows] = q_ref[:, cols]
        d_all[rows] = d_ref[:, cols]
    key_index = lax.broadcasted_iota(jnp.int32, (window, ROWS), 0)
    row_index = lax.broadcasted_iota(jnp.int32, (window, ROWS), 1)
    allowed = (key_index >= start_ref[...] - first) & (key_index <= row_index + reach)
    bias = jnp.where(allowed, 0.0, -1e30)
    scores = lax.dot_general(keys, q_all[...], NT, preferred_element_type=jnp.float32)
    gprobs = lax.dot_general(vals, d_all[...], NT, preferred_element_type=jnp.float32)
    for j in range(REP):
        cols = slice(j * HD, (j + 1) * HD)
        dots = jnp.sum(
            jnp.transpose(
                o_ref[:, cols].astype(jnp.float32) * d_ref[:, cols].astype(jnp.float32)
            ),
            axis=0,
            keepdims=True,
        )
        weights = jnp.exp2(scores[:, cols] * (SCALE * math.log2(math.e)) + bias)
        inverse = 1.0 / jnp.sum(weights, axis=0, keepdims=True)
        probs = weights * inverse
        pt[:, cols] = probs.astype(jnp.bfloat16)
        dst[:, cols] = (probs * (gprobs[:, cols] - dots)).astype(jnp.bfloat16)
    acc[1, pl.ds(first, window)] += jnp.dot(
        pt[...], d_all[...], preferred_element_type=jnp.float32
    )
    acc[0, pl.ds(first, window)] += jnp.dot(
        dst[...], q_all[...], preferred_element_type=jnp.float32
    )
    rot = jnp.dot(jnp.transpose(keys), dst[...], preferred_element_type=jnp.float32)
    half = HD // 2
    cosine = cos_ref[...] * SCALE
    sine = sin_ref[...] * SCALE
    for j in range(REP):
        cols = slice(j * HD, (j + 1) * HD)
        upper = rot[:half, cols]
        lower = rot[half:, cols]
        turned = jnp.concatenate(
            [upper * cosine + lower * sine, lower * cosine - upper * sine], axis=0
        )
        dq_ref[:, cols] = jnp.transpose(turned).astype(jnp.bfloat16)

    @pl.when(last_step)
    def _():
        for side, factor in ((0, SCALE), (1, 1.0)):
            pair_out[group, side] = (acc[side, count : 2 * count] * factor).astype(jnp.bfloat16)
            back_out[group, side] = (acc[side, 0:count] * factor).astype(jnp.bfloat16)
            own_acc[group, side] = acc[side, 2 * count :] * factor

        @pl.when(me >= 1)
        def _():
            pair_copy(group).start()

        @pl.when(even & has_before)
        def _():
            back_copy(group).start()

        @pl.when(odd & has_before & (group >= 1))
        def _():
            relay_back(group - 1)

        @pl.when(group >= 2)
        def _():
            finish(group - 2)

    @pl.when(last_step & (group == G - 1))
    def _():
        @pl.when(odd & has_before)
        def _():
            relay_back(G - 1)

        finish(G - 2)
        finish(G - 1)

        for f in range(seqs):
            rows = slice(f * count, (f + 1) * count)

            @pl.when(seq == f)
            def _():
                both_ref[rows, 0:HD] = done_out[f, 0]
                both_ref[rows, HD:] = done_out[f, 1]

            @pl.when(seq != f)
            def _():
                done_arrival(f).wait_recv()
                both_ref[rows, 0:HD] = done_in[f, 0]
                both_ref[rows, HD:] = done_in[f, 1]
                done_arrival(f).wait_send()

        for g in range(G):

            @pl.when(has_after)
            def _():
                far_copy(g).wait_send()

            @pl.when(even | has_before)
            def _():
                near_own(g).wait_send()

            @pl.when(me >= 1)
            def _():
                pair_copy(g).wait_send()

            @pl.when(has_before)
            def _():
                back_copy(g).wait_send()


def attention(start, cos_t, sin_t, key_cos, key_sin, q, o, d, k, v, seqs):
    count = q.shape[0]
    steps = count // ROWS
    window = SPAN * count + ROWS
    half = HD // 2
    by_step = lambda g, i: (0, i)
    fixed = lambda g, i: (0, 0)
    wide = pl.BlockSpec((ROWS, REP * HD), lambda g, i: (i, g))
    rows = pl.BlockSpec((count, G * HD), fixed)
    table = pl.BlockSpec((count, HD), fixed)
    flops = G * steps * 5 * 2 * window * REP * ROWS * HD
    slots = pltpu.VMEM((G, 2, count, HD), jnp.bfloat16)
    sems = pltpu.SemaphoreType.DMA((2, G))
    assert seqs == G
    return pl.pallas_call(
        attention_kernel,
        grid=(G, steps),
        in_specs=[
            pl.BlockSpec((1, ROWS), by_step),
            pl.BlockSpec((half, ROWS), by_step),
            pl.BlockSpec((half, ROWS), by_step),
            table, table, wide, wide, wide, rows, rows,
        ],
        out_specs=[wide, pl.BlockSpec((seqs * count, 2 * HD), fixed)],
        out_shape=[
            jax.ShapeDtypeStruct((count, H * HD), jnp.bfloat16),
            jax.ShapeDtypeStruct((seqs * count, 2 * HD), jnp.bfloat16),
        ],
        scratch_shapes=[
            pltpu.VMEM(((SPAN + 1) * count, HD), jnp.bfloat16),
            pltpu.VMEM(((SPAN + 1) * count, HD), jnp.bfloat16),
            pltpu.VMEM((REP * ROWS, HD), jnp.bfloat16),
            pltpu.VMEM((REP * ROWS, HD), jnp.bfloat16),
            pltpu.VMEM((window, REP * ROWS), jnp.bfloat16),
            pltpu.VMEM((window, REP * ROWS), jnp.bfloat16),
            pltpu.VMEM((2, (SPAN + 1) * count, HD), jnp.float32),
            slots, slots, slots, slots, slots, slots, slots,
            pltpu.VMEM((G, 2, count, HD), jnp.float32),
            slots, slots,
            sems, sems, sems, sems, sems,
        ],
        compiler_params=pltpu.CompilerParams(
            vmem_limit_bytes=48 << 20, collective_id=0, has_side_effects=True
        ),
        cost_estimate=pl.CostEstimate(
            flops=2 * flops, bytes_accessed=16 << 20, transcendentals=steps * G * window * REP * ROWS
        ),
    )(start, cos_t, sin_t, key_cos, key_sin, q, o, d, k, v)


def reduce_kernel(
    term_ref, out_ref, paired, mine, got, send_one, recv_one, send_two, recv_two
):
    peers = term_ref.shape[0]
    half = peers // 2
    me = lax.axis_index("ctx")
    parity = lax.rem(me, 2)
    spot = lax.div(me, 2)
    pair = me + 1 - 2 * parity
    barrier = pltpu.get_barrier_semaphore()
    pl.semaphore_signal(
        barrier, inc=1, device_id={"ctx": pair}, device_id_type=pl.DeviceIdType.MESH
    )
    for k in range(half - 1):
        other = 2 * lax.rem(spot + k + 1, half) + parity
        pl.semaphore_signal(
            barrier, inc=1, device_id={"ctx": other}, device_id_type=pl.DeviceIdType.MESH
        )
    pl.semaphore_wait(barrier, half)
    firsts = []
    for k in range(half):
        target = lax.rem(spot + k + 1, half)
        copy = pltpu.make_async_remote_copy(
            src_ref=term_ref.at[2 * target + 1 - parity],
            dst_ref=paired.at[k],
            send_sem=send_one.at[k],
            recv_sem=recv_one.at[k],
            device_id={"ctx": pair},
            device_id_type=pl.DeviceIdType.MESH,
        )
        copy.start()
        firsts.append(copy)
    seconds = []
    total = None
    for k in range(half):
        target = lax.rem(spot + k + 1, half)
        firsts[k].wait_recv()
        summed = term_ref[2 * target + parity].astype(jnp.float32) + paired[k].astype(
            jnp.float32
        )
        if k == half - 1:
            out_ref[...] = summed
            break
        mine[k] = summed.astype(jnp.bfloat16)
        copy = pltpu.make_async_remote_copy(
            src_ref=mine.at[k],
            dst_ref=got.at[k],
            send_sem=send_two.at[k],
            recv_sem=recv_two.at[k],
            device_id={"ctx": 2 * target + parity},
            device_id_type=pl.DeviceIdType.MESH,
        )
        copy.start()
        seconds.append(copy)
    for copy in seconds:
        copy.wait_recv()
    total = out_ref[...]
    for k in range(half - 1):
        total = total + got[k].astype(jnp.float32)
    out_ref[...] = total
    for copy in firsts + seconds:
        copy.wait_send()


def reduced(term, peers):
    rows, width = term.shape[0] // peers, term.shape[1]
    half = peers // 2
    whole = pl.BlockSpec(memory_space=pltpu.VMEM)
    return pl.pallas_call(
        reduce_kernel,
        in_specs=[whole],
        out_specs=whole,
        out_shape=jax.ShapeDtypeStruct((rows, width), jnp.float32),
        scratch_shapes=[
            pltpu.VMEM((half, rows, width), jnp.bfloat16),
            pltpu.VMEM((half - 1, rows, width), jnp.bfloat16),
            pltpu.VMEM((half - 1, rows, width), jnp.bfloat16),
            pltpu.SemaphoreType.DMA((half,)),
            pltpu.SemaphoreType.DMA((half,)),
            pltpu.SemaphoreType.DMA((half - 1,)),
            pltpu.SemaphoreType.DMA((half - 1,)),
        ],
        compiler_params=pltpu.CompilerParams(collective_id=1, has_side_effects=True),
    )(term.reshape(peers, rows, width))


def product_kernel(
    li_ref, both_ref, out_ref,
    turned, li_buf, term_wide, term, paired, mine, got,
    li_sems, send_one, recv_one, send_two, recv_two,
):
    half, _, rows, _ = term.shape
    me = lax.axis_index("ctx")
    parity = lax.rem(me, 2)
    spot = lax.div(me, 2)
    pair = me + 1 - 2 * parity
    loads = []
    for k in range(half):
        target = lax.rem(spot + k + 1, half)
        first = pl.multiple_of(target * (2 * rows), 128)
        load = pltpu.make_async_copy(
            li_ref.at[:, pl.ds(first, 2 * rows)], li_buf.at[k], li_sems.at[k]
        )
        load.start()
        loads.append(load)
    barrier = pltpu.get_barrier_semaphore()
    pl.semaphore_signal(
        barrier, inc=1, device_id={"ctx": pair}, device_id_type=pl.DeviceIdType.MESH
    )
    for k in range(half - 1):
        other = 2 * lax.rem(spot + k + 1, half) + parity
        pl.semaphore_signal(
            barrier, inc=1, device_id={"ctx": other}, device_id_type=pl.DeviceIdType.MESH
        )
    turned[...] = jnp.transpose(both_ref[...])
    pl.semaphore_wait(barrier, half)
    firsts = []
    seconds = []

    def pass_on(k):
        target = lax.rem(spot + k + 1, half)
        firsts[k].wait_recv()
        summed = term_wide[k, parity] + paired[k].astype(jnp.float32)
        if k == half - 1:
            out_ref[...] = summed
            return
        mine[k] = summed.astype(jnp.bfloat16)
        copy = pltpu.make_async_remote_copy(
            src_ref=mine.at[k],
            dst_ref=got.at[k],
            send_sem=send_two.at[k],
            recv_sem=recv_two.at[k],
            device_id={"ctx": 2 * target + parity},
            device_id_type=pl.DeviceIdType.MESH,
        )
        copy.start()
        seconds.append(copy)

    for k in range(half):
        loads[k].wait()
        product = jnp.transpose(
            jnp.dot(turned[...], li_buf[k], preferred_element_type=jnp.float32)
        )
        for side in range(2):
            piece = product[side * rows : (side + 1) * rows]
            term_wide[k, side] = piece
            term[k, side] = piece.astype(jnp.bfloat16)
        copy = pltpu.make_async_remote_copy(
            src_ref=term.at[k, 1 - parity],
            dst_ref=paired.at[k],
            send_sem=send_one.at[k],
            recv_sem=recv_one.at[k],
            device_id={"ctx": pair},
            device_id_type=pl.DeviceIdType.MESH,
        )
        copy.start()
        firsts.append(copy)
    for k in range(half):
        pass_on(k)
    for copy in seconds:
        copy.wait_recv()
    total = out_ref[...]
    for k in range(half - 1):
        total = total + got[k].astype(jnp.float32)
    out_ref[...] = total
    for copy in firsts + seconds:
        copy.wait_send()


def product_reduced(inputs, both, peers):
    depth, width = both.shape
    rows = inputs.shape[1] // peers
    half = peers // 2
    return pl.pallas_call(
        product_kernel,
        in_specs=[
            pl.BlockSpec(memory_space=pl.ANY),
            pl.BlockSpec(memory_space=pltpu.VMEM),
        ],
        out_specs=pl.BlockSpec(memory_space=pltpu.VMEM),
        out_shape=jax.ShapeDtypeStruct((rows, width), jnp.float32),
        scratch_shapes=[
            pltpu.VMEM((width, depth), jnp.bfloat16),
            pltpu.VMEM((half, depth, 2 * rows), jnp.bfloat16),
            pltpu.VMEM((half, 2, rows, width), jnp.float32),
            pltpu.VMEM((half, 2, rows, width), jnp.bfloat16),
            pltpu.VMEM((half, rows, width), jnp.bfloat16),
            pltpu.VMEM((half - 1, rows, width), jnp.bfloat16),
            pltpu.VMEM((half - 1, rows, width), jnp.bfloat16),
            pltpu.SemaphoreType.DMA((half,)),
            pltpu.SemaphoreType.DMA((half,)),
            pltpu.SemaphoreType.DMA((half,)),
            pltpu.SemaphoreType.DMA((half - 1,)),
            pltpu.SemaphoreType.DMA((half - 1,)),
        ],
        compiler_params=pltpu.CompilerParams(
            vmem_limit_bytes=48 << 20, collective_id=1, has_side_effects=True
        ),
    )(inputs, both)


def on_device(queries, keys_rot, values, attention_out, grad_out, layer_input, doc_lengths):
    k_rows = keys_rot[0]
    v_rows = values[0]
    lengths = doc_lengths[0]
    count = k_rows.shape[0]
    shard = lax.axis_index("ctx")
    inputs = lax.all_gather(layer_input[0], "fsdp", axis=0, tiled=True)
    place = shard * count + jnp.arange(count, dtype=jnp.int32)
    starts = jnp.cumsum(lengths) - lengths
    start = jnp.max(jnp.where(starts[:, None] <= place[None, :], starts[:, None], 0), axis=0)
    local = (place - start).astype(jnp.float32)
    half = HD // 2
    inverse_freq = jnp.power(
        jnp.float32(1000000.0), -(jnp.arange(half, dtype=jnp.float32) * 2.0 / HD)
    )
    angles = inverse_freq[:, None] * local[None, :]
    cos_t = jnp.cos(angles)
    sin_t = jnp.sin(angles)
    relative = (start - (shard - SPAN) * count)[None, :]
    key_cos = jnp.concatenate([cos_t.T, cos_t.T], axis=1)
    key_sin = jnp.concatenate([sin_t.T, -sin_t.T], axis=1)
    dq, both = attention(
        relative, cos_t, sin_t, key_cos, key_sin, queries[0], attention_out[0], grad_out[0],
        k_rows, v_rows, lax.axis_size("fsdp"),
    )
    peers = lax.axis_size("ctx")
    if (2 * DW // peers) % 128 == 0:
        summed = product_reduced(inputs, both, peers)
    else:
        term = lax.dot_general(
            inputs, both, (((0,), (0,)), ((), ())), preferred_element_type=jnp.float32
        )
        summed = reduced(term.astype(jnp.bfloat16), peers)
    width = summed.shape[1] // 2
    return (dq[None], summed[:, :width], summed[:, width:])


def solution(mesh):
    in_specs = (
        P("fsdp", "ctx", None),
        P("fsdp", "ctx", None),
        P("fsdp", "ctx", None),
        P("fsdp", "ctx", None),
        P("fsdp", "ctx", None),
        P("fsdp", "ctx", None),
        P("fsdp", None),
    )
    out_specs = (P("fsdp", "ctx", None), P("ctx", "fsdp"), P("ctx", "fsdp"))
    return jax.shard_map(
        on_device, mesh=mesh, in_specs=in_specs, out_specs=out_specs, check_vma=False
    )
```

```python
import math

import jax
import jax.numpy as jnp
from jax import lax
from jax.experimental import pallas as pl
from jax.experimental.pallas import tpu as pltpu
from jax.sharding import PartitionSpec as P

H = 20
G = 4
HD = 128
REP = H // G
DW = 2560
SPAN = 2
ROWS = 128
SCALE = 1.0 / math.sqrt(HD)
NT = (((1,), (1,)), ((), ()))


def attention_kernel(
    start_ref, cos_ref, sin_ref, key_cos_ref, key_sin_ref, q_ref, o_ref, d_ref, k_ref, v_ref, li_ref,
    dq_ref, both_ref, li_all,
    kwin, vwin, q_all, d_all, pt, dst, acc,
    own_kv, far_kv, near_kv, pair_out, pair_in, back_out, back_in, own_acc, done_out, done_in,
    far_sems, near_sems, pair_sems, back_sems, done_sems, cross_sems, pass_sems, core_sems,
    local_sem,
):
    group = pl.program_id(0)
    step = pl.program_id(1)
    count = k_ref.shape[0]
    reach = SPAN * count
    window = reach + ROWS
    peers = lax.axis_size("ctx")
    seqs = lax.axis_size("fsdp")
    me = lax.axis_index("ctx")
    seq = lax.axis_index("fsdp")
    odd = lax.rem(me, 2) == 1
    even = lax.rem(me, 2) == 0
    pair = me + 1 - 2 * lax.rem(me, 2)
    has_before = me >= 2
    has_after = me < peers - 2
    first_step = step == 0
    last_step = step == pl.num_programs(1) - 1

    def remote(src, dst_buf, sems, index, where):
        return pltpu.make_async_remote_copy(
            src_ref=src,
            dst_ref=dst_buf,
            send_sem=sems.at[0, index],
            recv_sem=sems.at[1, index],
            device_id=where,
            device_id_type=pl.DeviceIdType.MESH,
        )

    def far_copy(g):
        return remote(own_kv.at[g], far_kv.at[g], far_sems, g, {"ctx": me + 2})

    def near_own(g):
        return remote(own_kv.at[g], near_kv.at[g], near_sems, g, {"ctx": pair})

    def near_relay(g):
        return remote(far_kv.at[g], near_kv.at[g], near_sems, g, {"ctx": pair})

    def pair_copy(g):
        return remote(pair_out.at[g], pair_in.at[g], pair_sems, g, {"ctx": pair})

    def back_copy(g):
        return remote(back_out.at[g], back_in.at[g], back_sems, g, {"ctx": me - 2})

    def done_copy(g):
        return pltpu.make_async_remote_copy(
            src_ref=done_out.at[g],
            dst_ref=done_in.at[seq],
            send_sem=done_sems.at[0, g],
            recv_sem=done_sems.at[1, seq],
            device_id={"fsdp": g},
            device_id_type=pl.DeviceIdType.MESH,
        )

    def done_arrival(f):
        return pltpu.make_async_remote_copy(
            src_ref=done_out.at[f],
            dst_ref=done_in.at[f],
            send_sem=done_sems.at[0, f],
            recv_sem=done_sems.at[1, f],
            device_id={"fsdp": f},
            device_id_type=pl.DeviceIdType.MESH,
        )

    core = seq + 1 - 2 * lax.rem(seq, 2)
    across = lax.rem(seq + 2, seqs)
    piece = count // G

    def core_copy():
        return remote(li_ref, li_all.at[seq], core_sems, 0, {"fsdp": core})

    def local_copy():
        return pltpu.make_async_copy(li_ref, li_all.at[seq], local_sem)

    def cross_copy(g):
        rows = pl.ds(g * piece, piece)
        return remote(
            li_ref.at[rows], li_all.at[seq, rows], cross_sems, g, {"fsdp": across}
        )

    def pass_copy(g):
        part = li_all.at[across, pl.ds(g * piece, piece)]
        return remote(part, part, pass_sems, g, {"fsdp": core})

    def pass_across(g):
        cross_copy(g).wait_recv()
        pass_copy(g).start()

    def relay_near(g):
        far_copy(g).wait_recv()
        near_relay(g).start()

    def relay_back(g):
        pair_copy(g).wait_recv()
        back_out[g] = (
            back_out[g].astype(jnp.float32) + pair_in[g].astype(jnp.float32)
        ).astype(jnp.bfloat16)
        back_copy(g).start()

    def finish(g):
        @pl.when(even)
        def _():
            pair_copy(g).wait_recv()
            own_acc[g] += pair_in[g].astype(jnp.float32)

        @pl.when(has_after)
        def _():
            back_copy(g).wait_recv()
            own_acc[g] += back_in[g].astype(jnp.float32)

        keyed = own_acc[g, 0]
        turned = keyed * key_cos_ref[...] + pltpu.roll(keyed, HD // 2, 1) * key_sin_ref[...]
        done_out[g, 0] = turned.astype(jnp.bfloat16)
        done_out[g, 1] = own_acc[g, 1].astype(jnp.bfloat16)

        @pl.when(seq != g)
        def _():
            done_copy(g).start()

    @pl.when(first_step & (group == 0))
    def _():
        barrier = pltpu.get_barrier_semaphore()

        def greet(where):
            pl.semaphore_signal(
                barrier, inc=1, device_id=where, device_id_type=pl.DeviceIdType.MESH
            )

        greet({"ctx": pair})
        for k in range(1, seqs):
            greet({"fsdp": lax.rem(seq + k, seqs)})

        @pl.when(has_after)
        def _():
            greet({"ctx": me + 2})

        @pl.when(has_before)
        def _():
            greet({"ctx": me - 2})

        for g in range(G):
            own_kv[g, 0] = k_ref[:, g * HD : (g + 1) * HD]
            own_kv[g, 1] = v_ref[:, g * HD : (g + 1) * HD]
        @pl.when(has_after & has_before)
        def _():
            pl.semaphore_wait(barrier, seqs + 2)

        @pl.when(jnp.logical_not(has_after & has_before))
        def _():
            pl.semaphore_wait(barrier, seqs + 1)

        for g in range(G):

            @pl.when(has_after)
            def _():
                far_copy(g).start()

            @pl.when(even)
            def _():
                near_own(g).start()

        for g in range(G):
            cross_copy(g).start()
        core_copy().start()
        local_copy().start()

        @pl.when(odd & has_before)
        def _():
            relay_near(0)

    @pl.when(first_step & odd & has_before & (group < G - 1))
    def _():
        relay_near(group + 1)

    @pl.when(first_step)
    def _():
        kwin[2 * count :] = own_kv[group, 0]
        vwin[2 * count :] = own_kv[group, 1]
        acc[...] = jnp.zeros_like(acc)

        @pl.when(even & has_before)
        def _():
            far_copy(group).wait_recv()

        @pl.when(has_before)
        def _():
            kwin[0:count] = far_kv[group, 0]
            vwin[0:count] = far_kv[group, 1]

        @pl.when(me < 2)
        def _():
            kwin[0:count] = jnp.zeros((count, HD), jnp.bfloat16)
            vwin[0:count] = jnp.zeros((count, HD), jnp.bfloat16)

        @pl.when(me >= 1)
        def _():
            near_own(group).wait_recv()
            kwin[count : 2 * count] = near_kv[group, 0]
            vwin[count : 2 * count] = near_kv[group, 1]

        @pl.when(me < 1)
        def _():
            kwin[count : 2 * count] = jnp.zeros((count, HD), jnp.bfloat16)
            vwin[count : 2 * count] = jnp.zeros((count, HD), jnp.bfloat16)

    first = pl.multiple_of(step * ROWS, ROWS)
    keys = kwin[pl.ds(first, window)]
    vals = vwin[pl.ds(first, window)]
    for j in range(REP):
        cols = slice(j * HD, (j + 1) * HD)
        rows = slice(j * ROWS, (j + 1) * ROWS)
        q_all[rows] = q_ref[:, cols]
        d_all[rows] = d_ref[:, cols]
    key_index = lax.broadcasted_iota(jnp.int32, (window, ROWS), 0)
    row_index = lax.broadcasted_iota(jnp.int32, (window, ROWS), 1)
    allowed = (key_index >= start_ref[...] - first) & (key_index <= row_index + reach)
    bias = jnp.where(allowed, 0.0, -1e30)
    scores = lax.dot_general(keys, q_all[...], NT, preferred_element_type=jnp.float32)
    gprobs = lax.dot_general(vals, d_all[...], NT, preferred_element_type=jnp.float32)
    for j in range(REP):
        cols = slice(j * HD, (j + 1) * HD)
        dots = jnp.sum(
            jnp.transpose(
                o_ref[:, cols].astype(jnp.float32) * d_ref[:, cols].astype(jnp.float32)
            ),
            axis=0,
            keepdims=True,
        )
        weights = jnp.exp2(scores[:, cols] * (SCALE * math.log2(math.e)) + bias)
        inverse = 1.0 / jnp.sum(weights, axis=0, keepdims=True)
        probs = weights * inverse
        pt[:, cols] = probs.astype(jnp.bfloat16)
        dst[:, cols] = (probs * (gprobs[:, cols] - dots)).astype(jnp.bfloat16)
    acc[1, pl.ds(first, window)] += jnp.dot(
        pt[...], d_all[...], preferred_element_type=jnp.float32
    )
    acc[0, pl.ds(first, window)] += jnp.dot(
        dst[...], q_all[...], preferred_element_type=jnp.float32
    )
    rot = jnp.dot(jnp.transpose(keys), dst[...], preferred_element_type=jnp.float32)
    half = HD // 2
    cosine = cos_ref[...] * SCALE
    sine = sin_ref[...] * SCALE
    for j in range(REP):
        cols = slice(j * HD, (j + 1) * HD)
        upper = rot[:half, cols]
        lower = rot[half:, cols]
        turned = jnp.concatenate(
            [upper * cosine + lower * sine, lower * cosine - upper * sine], axis=0
        )
        dq_ref[:, cols] = jnp.transpose(turned).astype(jnp.bfloat16)

    @pl.when(last_step)
    def _():
        for side, factor in ((0, SCALE), (1, 1.0)):
            pair_out[group, side] = (acc[side, count : 2 * count] * factor).astype(jnp.bfloat16)
            back_out[group, side] = (acc[side, 0:count] * factor).astype(jnp.bfloat16)
            own_acc[group, side] = acc[side, 2 * count :] * factor

        @pl.when(me >= 1)
        def _():
            pair_copy(group).start()

        @pl.when(even & has_before)
        def _():
            back_copy(group).start()

        @pl.when(odd & has_before & (group >= 1))
        def _():
            relay_back(group - 1)

        @pl.when(group >= 1)
        def _():
            pass_across(group - 1)

        @pl.when(group >= 2)
        def _():
            finish(group - 2)

    @pl.when(last_step & (group == G - 1))
    def _():
        @pl.when(odd & has_before)
        def _():
            relay_back(G - 1)

        finish(G - 2)
        pass_across(G - 1)
        finish(G - 1)

        for f in range(seqs):
            rows = slice(f * count, (f + 1) * count)

            @pl.when(seq == f)
            def _():
                both_ref[rows, 0:HD] = done_out[f, 0]
                both_ref[rows, HD:] = done_out[f, 1]

            @pl.when(seq != f)
            def _():
                done_arrival(f).wait_recv()
                both_ref[rows, 0:HD] = done_in[f, 0]
                both_ref[rows, HD:] = done_in[f, 1]
                done_arrival(f).wait_send()

        for g in range(G):

            @pl.when(has_after)
            def _():
                far_copy(g).wait_send()

            @pl.when(even | has_before)
            def _():
                near_own(g).wait_send()

            @pl.when(me >= 1)
            def _():
                pair_copy(g).wait_send()

            @pl.when(has_before)
            def _():
                back_copy(g).wait_send()

            cross_copy(g).wait_send()
            pass_copy(g).wait()

        core_copy().wait()
        local_copy().wait()


def attention(start, cos_t, sin_t, key_cos, key_sin, q, o, d, k, v, li, seqs):
    count = q.shape[0]
    steps = count // ROWS
    window = SPAN * count + ROWS
    half = HD // 2
    by_step = lambda g, i: (0, i)
    fixed = lambda g, i: (0, 0)
    wide = pl.BlockSpec((ROWS, REP * HD), lambda g, i: (i, g))
    rows = pl.BlockSpec((count, G * HD), fixed)
    table = pl.BlockSpec((count, HD), fixed)
    flops = G * steps * 5 * 2 * window * REP * ROWS * HD
    slots = pltpu.VMEM((G, 2, count, HD), jnp.bfloat16)
    sems = pltpu.SemaphoreType.DMA((2, G))
    assert seqs == G
    return pl.pallas_call(
        attention_kernel,
        grid=(G, steps),
        in_specs=[
            pl.BlockSpec((1, ROWS), by_step),
            pl.BlockSpec((half, ROWS), by_step),
            pl.BlockSpec((half, ROWS), by_step),
            table, table, wide, wide, wide, rows, rows,
            pl.BlockSpec(memory_space=pl.ANY),
        ],
        out_specs=[
            wide,
            pl.BlockSpec((seqs * count, 2 * HD), fixed),
            pl.BlockSpec(memory_space=pl.ANY),
        ],
        out_shape=[
            jax.ShapeDtypeStruct((count, H * HD), jnp.bfloat16),
            jax.ShapeDtypeStruct((seqs * count, 2 * HD), jnp.bfloat16),
            jax.ShapeDtypeStruct((seqs, count, li.shape[1]), li.dtype),
        ],
        scratch_shapes=[
            pltpu.VMEM(((SPAN + 1) * count, HD), jnp.bfloat16),
            pltpu.VMEM(((SPAN + 1) * count, HD), jnp.bfloat16),
            pltpu.VMEM((REP * ROWS, HD), jnp.bfloat16),
            pltpu.VMEM((REP * ROWS, HD), jnp.bfloat16),
            pltpu.VMEM((window, REP * ROWS), jnp.bfloat16),
            pltpu.VMEM((window, REP * ROWS), jnp.bfloat16),
            pltpu.VMEM((2, (SPAN + 1) * count, HD), jnp.float32),
            slots, slots, slots, slots, slots, slots, slots,
            pltpu.VMEM((G, 2, count, HD), jnp.float32),
            slots, slots,
            sems, sems, sems, sems, sems, sems, sems,
            pltpu.SemaphoreType.DMA((2, 1)),
            pltpu.SemaphoreType.DMA,
        ],
        compiler_params=pltpu.CompilerParams(
            vmem_limit_bytes=48 << 20, collective_id=0, has_side_effects=True
        ),
        cost_estimate=pl.CostEstimate(
            flops=2 * flops, bytes_accessed=16 << 20, transcendentals=steps * G * window * REP * ROWS
        ),
    )(start, cos_t, sin_t, key_cos, key_sin, q, o, d, k, v, li)


def reduce_kernel(
    term_ref, out_ref, paired, mine, got, send_one, recv_one, send_two, recv_two
):
    peers = term_ref.shape[0]
    half = peers // 2
    me = lax.axis_index("ctx")
    parity = lax.rem(me, 2)
    spot = lax.div(me, 2)
    pair = me + 1 - 2 * parity
    barrier = pltpu.get_barrier_semaphore()
    pl.semaphore_signal(
        barrier, inc=1, device_id={"ctx": pair}, device_id_type=pl.DeviceIdType.MESH
    )
    for k in range(half - 1):
        other = 2 * lax.rem(spot + k + 1, half) + parity
        pl.semaphore_signal(
            barrier, inc=1, device_id={"ctx": other}, device_id_type=pl.DeviceIdType.MESH
        )
    pl.semaphore_wait(barrier, half)
    firsts = []
    for k in range(half):
        target = lax.rem(spot + k + 1, half)
        copy = pltpu.make_async_remote_copy(
            src_ref=term_ref.at[2 * target + 1 - parity],
            dst_ref=paired.at[k],
            send_sem=send_one.at[k],
            recv_sem=recv_one.at[k],
            device_id={"ctx": pair},
            device_id_type=pl.DeviceIdType.MESH,
        )
        copy.start()
        firsts.append(copy)
    seconds = []
    total = None
    for k in range(half):
        target = lax.rem(spot + k + 1, half)
        firsts[k].wait_recv()
        summed = term_ref[2 * target + parity].astype(jnp.float32) + paired[k].astype(
            jnp.float32
        )
        if k == half - 1:
            out_ref[...] = summed
            break
        mine[k] = summed.astype(jnp.bfloat16)
        copy = pltpu.make_async_remote_copy(
            src_ref=mine.at[k],
            dst_ref=got.at[k],
            send_sem=send_two.at[k],
            recv_sem=recv_two.at[k],
            device_id={"ctx": 2 * target + parity},
            device_id_type=pl.DeviceIdType.MESH,
        )
        copy.start()
        seconds.append(copy)
    for copy in seconds:
        copy.wait_recv()
    total = out_ref[...]
    for k in range(half - 1):
        total = total + got[k].astype(jnp.float32)
    out_ref[...] = total
    for copy in firsts + seconds:
        copy.wait_send()


def reduced(term, peers):
    rows, width = term.shape[0] // peers, term.shape[1]
    half = peers // 2
    whole = pl.BlockSpec(memory_space=pltpu.VMEM)
    return pl.pallas_call(
        reduce_kernel,
        in_specs=[whole],
        out_specs=whole,
        out_shape=jax.ShapeDtypeStruct((rows, width), jnp.float32),
        scratch_shapes=[
            pltpu.VMEM((half, rows, width), jnp.bfloat16),
            pltpu.VMEM((half - 1, rows, width), jnp.bfloat16),
            pltpu.VMEM((half - 1, rows, width), jnp.bfloat16),
            pltpu.SemaphoreType.DMA((half,)),
            pltpu.SemaphoreType.DMA((half,)),
            pltpu.SemaphoreType.DMA((half - 1,)),
            pltpu.SemaphoreType.DMA((half - 1,)),
        ],
        compiler_params=pltpu.CompilerParams(collective_id=1, has_side_effects=True),
    )(term.reshape(peers, rows, width))


def product_kernel(
    li_ref, both_ref, out_ref,
    turned, li_buf, term_wide, term, paired, mine, got,
    li_sems, send_one, recv_one, send_two, recv_two,
):
    half, _, rows, _ = term.shape
    me = lax.axis_index("ctx")
    parity = lax.rem(me, 2)
    spot = lax.div(me, 2)
    pair = me + 1 - 2 * parity
    loads = []
    for k in range(half):
        target = lax.rem(spot + k + 1, half)
        first = pl.multiple_of(target * (2 * rows), 128)
        load = pltpu.make_async_copy(
            li_ref.at[:, pl.ds(first, 2 * rows)], li_buf.at[k], li_sems.at[k]
        )
        load.start()
        loads.append(load)
    barrier = pltpu.get_barrier_semaphore()
    pl.semaphore_signal(
        barrier, inc=1, device_id={"ctx": pair}, device_id_type=pl.DeviceIdType.MESH
    )
    for k in range(half - 1):
        other = 2 * lax.rem(spot + k + 1, half) + parity
        pl.semaphore_signal(
            barrier, inc=1, device_id={"ctx": other}, device_id_type=pl.DeviceIdType.MESH
        )
    turned[...] = jnp.transpose(both_ref[...])
    pl.semaphore_wait(barrier, half)
    firsts = []
    seconds = []

    def pass_on(k):
        target = lax.rem(spot + k + 1, half)
        firsts[k].wait_recv()
        summed = term_wide[k, parity] + paired[k].astype(jnp.float32)
        if k == half - 1:
            out_ref[...] = summed
            return
        mine[k] = summed.astype(jnp.bfloat16)
        copy = pltpu.make_async_remote_copy(
            src_ref=mine.at[k],
            dst_ref=got.at[k],
            send_sem=send_two.at[k],
            recv_sem=recv_two.at[k],
            device_id={"ctx": 2 * target + parity},
            device_id_type=pl.DeviceIdType.MESH,
        )
        copy.start()
        seconds.append(copy)

    for k in range(half):
        loads[k].wait()
        product = jnp.transpose(
            jnp.dot(turned[...], li_buf[k], preferred_element_type=jnp.float32)
        )
        for side in range(2):
            piece = product[side * rows : (side + 1) * rows]
            term_wide[k, side] = piece
            term[k, side] = piece.astype(jnp.bfloat16)
        copy = pltpu.make_async_remote_copy(
            src_ref=term.at[k, 1 - parity],
            dst_ref=paired.at[k],
            send_sem=send_one.at[k],
            recv_sem=recv_one.at[k],
            device_id={"ctx": pair},
            device_id_type=pl.DeviceIdType.MESH,
        )
        copy.start()
        firsts.append(copy)
    for k in range(half):
        pass_on(k)
    for copy in seconds:
        copy.wait_recv()
    total = out_ref[...]
    for k in range(half - 1):
        total = total + got[k].astype(jnp.float32)
    out_ref[...] = total
    for copy in firsts + seconds:
        copy.wait_send()


def product_reduced(inputs, both, peers):
    depth, width = both.shape
    rows = inputs.shape[1] // peers
    half = peers // 2
    return pl.pallas_call(
        product_kernel,
        in_specs=[
            pl.BlockSpec(memory_space=pl.ANY),
            pl.BlockSpec(memory_space=pltpu.VMEM),
        ],
        out_specs=pl.BlockSpec(memory_space=pltpu.VMEM),
        out_shape=jax.ShapeDtypeStruct((rows, width), jnp.float32),
        scratch_shapes=[
            pltpu.VMEM((width, depth), jnp.bfloat16),
            pltpu.VMEM((half, depth, 2 * rows), jnp.bfloat16),
            pltpu.VMEM((half, 2, rows, width), jnp.float32),
            pltpu.VMEM((half, 2, rows, width), jnp.bfloat16),
            pltpu.VMEM((half, rows, width), jnp.bfloat16),
            pltpu.VMEM((half - 1, rows, width), jnp.bfloat16),
            pltpu.VMEM((half - 1, rows, width), jnp.bfloat16),
            pltpu.SemaphoreType.DMA((half,)),
            pltpu.SemaphoreType.DMA((half,)),
            pltpu.SemaphoreType.DMA((half,)),
            pltpu.SemaphoreType.DMA((half - 1,)),
            pltpu.SemaphoreType.DMA((half - 1,)),
        ],
        compiler_params=pltpu.CompilerParams(
            vmem_limit_bytes=48 << 20, collective_id=1, has_side_effects=True
        ),
    )(inputs, both)


def on_device(queries, keys_rot, values, attention_out, grad_out, layer_input, doc_lengths):
    k_rows = keys_rot[0]
    v_rows = values[0]
    lengths = doc_lengths[0]
    count = k_rows.shape[0]
    shard = lax.axis_index("ctx")
    place = shard * count + jnp.arange(count, dtype=jnp.int32)
    starts = jnp.cumsum(lengths) - lengths
    start = jnp.max(jnp.where(starts[:, None] <= place[None, :], starts[:, None], 0), axis=0)
    local = (place - start).astype(jnp.float32)
    half = HD // 2
    inverse_freq = jnp.power(
        jnp.float32(1000000.0), -(jnp.arange(half, dtype=jnp.float32) * 2.0 / HD)
    )
    angles = inverse_freq[:, None] * local[None, :]
    cos_t = jnp.cos(angles)
    sin_t = jnp.sin(angles)
    relative = (start - (shard - SPAN) * count)[None, :]
    key_cos = jnp.concatenate([cos_t.T, cos_t.T], axis=1)
    key_sin = jnp.concatenate([sin_t.T, -sin_t.T], axis=1)
    dq, both, inputs = attention(
        relative, cos_t, sin_t, key_cos, key_sin, queries[0], attention_out[0], grad_out[0],
        k_rows, v_rows, layer_input[0], lax.axis_size("fsdp"),
    )
    inputs = inputs.reshape(-1, DW)
    peers = lax.axis_size("ctx")
    if (2 * DW // peers) % 128 == 0:
        summed = product_reduced(inputs, both, peers)
    else:
        term = lax.dot_general(
            inputs, both, (((0,), (0,)), ((), ())), preferred_element_type=jnp.float32
        )
        summed = reduced(term.astype(jnp.bfloat16), peers)
    width = summed.shape[1] // 2
    return (dq[None], summed[:, :width], summed[:, width:])


def solution(mesh):
    in_specs = (
        P("fsdp", "ctx", None),
        P("fsdp", "ctx", None),
        P("fsdp", "ctx", None),
        P("fsdp", "ctx", None),
        P("fsdp", "ctx", None),
        P("fsdp", "ctx", None),
        P("fsdp", None),
    )
    out_specs = (P("fsdp", "ctx", None), P("ctx", "fsdp"), P("ctx", "fsdp"))
    return jax.shard_map(
        on_device, mesh=mesh, in_specs=in_specs, out_specs=out_specs, check_vma=False
    )
```
